32 devices in a mesh: wire: 16 (over z, y, x), col: 2 (over core).
Axes of the slice: x: 2, y: 2, z: 4, core: 2. Of those that a mesh axis runs over, the one named last changes fastest.
Arguments:
- hamiltonian: bfloat16 [256, 3, 128, 128], P('wire')
- offsets: int32 [256, 3], P('wire'), may hold values from -2 to 2, as said below
- phase_left: bfloat16 [32768, 2048], P('wire'), may hold values from -0.125 to 0.125
- phase_right: bfloat16 [32768, 2048], P('wire'), may hold values from -0.03125 to 0.03125
- orbitals: bfloat16 [32768, 512], P('wire', 'col'), may hold values from -6 to 6
Outputs:
- gradient: float32 [32768, 512], P('wire', 'col')
The draws below stay inside these ranges and needn't reach their ends.
Inputs may be any that keep to these rules, and one draw needn't show every extreme that they name: `offsets`: slot 0 of every row block has offset 0.
All inputs are finite; a program needn't handle non-finite values.
Results may differ from the reference program's by a relative error of at most 0.0017.
Values may be sent and summed in bfloat16 or wider, within the bound.
No kernel may reach another device: no remote copies, remote signals or barrier semaphores. Data moves between devices by JAX's collectives and lax.ppermute only.
A program may use at most 128 MiB of HBM per device.

```python
import jax
import jax.numpy as jnp
from jax import lax

B = 128
REACH = 2
SLOTS = 3
M = 512
K = 2048
NBLK = 256
ROWS = 32768


def draw_hamiltonian(key, part):
    noise_key = jax.random.fold_in(key, 11)
    site_key = jax.random.fold_in(key, 12)
    noise = jax.random.normal(noise_key, (NBLK, SLOTS, B, B), jnp.float32)
    noise = noise * (SLOTS * B) ** (-0.5)
    onsite = jax.random.uniform(site_key, (NBLK, B), jnp.float32, 0.5, 3.5)
    eye = jnp.eye(B, dtype=jnp.float32)
    first = noise[:, 0] + onsite[:, :, None] * eye[None]
    return jnp.concatenate([first[:, None], noise[:, 1:]], axis=1).astype(jnp.bfloat16)


def draw_offsets(key, part):
    drawn = jax.random.randint(jax.random.fold_in(key, 21), (NBLK, SLOTS - 1), 0 - REACH, REACH + 1, dtype=jnp.int32)
    drawn = drawn.at[0, 0].set(REACH).at[0, SLOTS - 2].set(0 - REACH)
    return jnp.concatenate([jnp.zeros((NBLK, 1), jnp.int32), drawn], axis=1)


def steps_of(key, dims, split, least, largest):
    factor_of = 1.0
    for position, shards_of in split:
        heights = jax.random.uniform(jax.random.fold_in(jax.random.fold_in(key, 6), position), (shards_of,), jnp.float32, least / len(split), largest / len(split))
        factor_of = factor_of * jnp.repeat(jnp.exp(heights), dims[position] // shards_of).reshape((-1,) + (1,) * (len(dims) - 1 - position))
    return factor_of


def normal_values(stream_key, dims, scale, reach, split=(), held_as=jnp.bfloat16):
    values = jax.random.normal(stream_key, dims, jnp.float32) * scale
    if len(split) > 0:
        values = steps_of(stream_key, dims, split, -0.22, 0.18) * values
    return jnp.clip(values, min=-reach, max=reach).astype(held_as)


def setup_inputs(seed: int = 0) -> dict:
    key_list = jax.random.split(jax.random.key(seed), 6)
    return {
        "hamiltonian": draw_hamiltonian(jax.random.fold_in(key_list[5], 71), 0),
        "offsets": draw_offsets(jax.random.fold_in(key_list[5], 71), 0),
        "phase_left": normal_values(key_list[2], (ROWS, K), K ** -0.5, 0.125, ((0, 16),)),
        "phase_right": normal_values(key_list[3], (ROWS, K), ROWS ** -0.5, 0.03125, ((0, 16),)),
        "orbitals": normal_values(key_list[4], (ROWS, M), 1.0, 6.0, ((0, 16), (1, 2))),
    }


def band_product(hamiltonian, offsets, orbitals):
    tiles = orbitals.reshape(NBLK, B, M).astype(jnp.float32)

    def one_block(packed):
        block_index, weights, shifts = packed
        picked = jnp.take(tiles, (block_index + shifts) % NBLK, axis=0)
        return jnp.einsum('sab,sbm->am', weights.astype(jnp.float32), picked)

    result = lax.map(one_block, (jnp.arange(NBLK, dtype=jnp.int32), hamiltonian, offsets))
    return result.reshape(ROWS, M)


def reference(hamiltonian, offsets, phase_left, phase_right, orbitals):
    band = band_product(hamiltonian, offsets, orbitals)
    coupling = jnp.dot(phase_right.T, orbitals, preferred_element_type=jnp.float32).astype(jnp.bfloat16)
    image = band + jnp.dot(phase_left, coupling, preferred_element_type=jnp.float32)
    wide = orbitals.astype(jnp.float32)
    intersection = jnp.dot(orbitals.T, orbitals, preferred_element_type=jnp.float32) / ROWS
    cross = jnp.dot(wide.T, image, precision=lax.Precision.HIGHEST) / ROWS
    gradient = 2.0 * image - jnp.dot(image, intersection, precision=lax.Precision.HIGHEST) - jnp.dot(wide, cross, precision=lax.Precision.HIGHEST)
    return gradient
```

```python
import math

import jax
import jax.numpy as jnp
from jax import lax
from jax.sharding import PartitionSpec as P

REACH = 2
F32 = jnp.float32
BF16 = jnp.bfloat16
F16 = jnp.float16


def split(value):
    high = lax.reduce_precision(value, 8, 7)
    return high.astype(BF16), (value - high).astype(BF16)


def dot_t(a, b):
    return lax.dot_general(a, b, (((0,), (0,)), ((), ())), preferred_element_type=F32)


def dot(a, b):
    return jnp.dot(a, b, preferred_element_type=F32)


class Cube:
    def __init__(self, chips, cores):
        count = chips.bit_length() - 1
        first = list(range(count))
        second = list(range(count))
        if count >= 3:
            first[1], first[2] = 2, 1
        if count >= 2:
            second[0], second[1] = 1, 0
        orders = (first, second)
        me = lax.axis_index("wire")
        core = lax.axis_index("col") % 2
        self.steps = []
        for k in range(count):
            perm = []
            for w in range(chips):
                for c in range(cores):
                    perm.append((w * cores + c, (w ^ (1 << orders[c % 2][k])) * cores + c))
            bit = (me >> jnp.where(core == 0, first[k], second[k])) & 1
            self.steps.append((perm, bit))

    def send(self, value, k):
        return lax.ppermute(value, ("wire", "col"), self.steps[k][0])

    def scatter(self, value, wire_type, steps):
        for k in steps:
            bit = self.steps[k][1]
            half = value.shape[0] // 2
            out = lax.dynamic_slice_in_dim(value, (1 - bit) * half, half, 0).astype(wire_type)
            got = self.send(out, k)
            value = lax.dynamic_slice_in_dim(value, bit * half, half, 0) + got.astype(F32)
        return value

    def gather(self, value, steps):
        for k in reversed(steps):
            bit = self.steps[k][1]
            got = self.send(value, k)
            value = jnp.where(
                bit == 0,
                jnp.concatenate([value, got], axis=0),
                jnp.concatenate([got, value], axis=0),
            )
        return value


def body(hamiltonian, offsets, phase_left, phase_right, orbitals):
    local_blocks = hamiltonian.shape[0]
    block_size = hamiltonian.shape[2]
    local_rows, cols = orbitals.shape
    rank = phase_left.shape[1]
    chips = lax.axis_size("wire")
    cores = lax.axis_size("col")
    total_rows = local_rows * chips
    cube = Cube(chips, cores)
    steps = list(range(len(cube.steps)))
    swap = [(i, (i + 1) % cores) for i in range(cores)]

    scale = 2.0 ** -max(0, math.ceil(math.log2(36.0 * total_rows / 32768.0)))
    coupling_part = dot_t(phase_right, orbitals)
    other = lax.ppermute(orbitals, "col", swap)
    own_part = dot_t(orbitals, orbitals) * scale
    other_part = dot_t(other, orbitals) * scale
    stacked = jnp.concatenate([coupling_part, own_part, other_part], axis=0)
    mine = cube.scatter(stacked, F16, steps)

    width = REACH * block_size
    up = [(i, (i + 1) % chips) for i in range(chips)]
    down = [(j, i) for i, j in up]
    before = lax.ppermute(orbitals[local_rows - width :], "wire", up)
    after = lax.ppermute(orbitals[:width], "wire", down)
    padded = jnp.concatenate([before, orbitals, after], axis=0)
    tiles = padded.reshape(local_blocks + 2 * REACH, block_size, cols)
    picks = jnp.arange(local_blocks, dtype=jnp.int32)[:, None] + offsets + REACH
    picked = jnp.take(tiles, picks, axis=0)
    band = jnp.einsum(
        "jsab,jsbm->jam", hamiltonian, picked, preferred_element_type=F32
    ).reshape(local_rows, cols)
    full = jnp.concatenate([orbitals, other], axis=1)
    band_high, band_low = split(band)
    cross_band = dot_t(full, band_high) + dot_t(full, band_low)
    left_high, left_low = split(dot_t(full, phase_left))

    piece = mine.shape[0]
    start = jnp.int32(0)
    span = stacked.shape[0]
    for _, bit in cube.steps:
        span //= 2
        start = start + bit * span
    row = start + lax.broadcasted_iota(jnp.int32, (piece, 1), 0)
    mine = jnp.where(row < rank, lax.reduce_precision(mine, 8, 7), mine).astype(F16)
    whole = cube.gather(mine, steps)
    coupling = whole[:rank].astype(BF16)
    inter_own = whole[rank : rank + cols].astype(F32) * (1.0 / (scale * total_rows))
    inter_other = whole[rank + cols :].astype(F32) * (1.0 / (scale * total_rows))

    cross_part = cross_band + dot(left_high, coupling) + dot(left_low, coupling)
    cross = cube.gather(cube.scatter(cross_part, F32, steps), steps) * (1.0 / total_rows)

    image = band + dot(phase_left, coupling)
    image_other = lax.ppermute(image, "col", swap)
    image_high, image_low = split(image)
    other_high, other_low = split(image_other)
    own_high, own_low = split(inter_own)
    cross_high, cross_low = split(inter_other)
    mixed = (
        dot(image_high, own_high)
        + dot(image_low, own_high)
        + dot(image_high, own_low)
        + dot(other_high, cross_high)
        + dot(other_low, cross_high)
        + dot(other_high, cross_low)
    )
    first = 2.0 * image - mixed
    high, low = split(cross)
    return first - (dot(full, high) + dot(full, low))


def solution(mesh):
    return jax.shard_map(
        body,
        mesh=mesh,
        in_specs=(
            P("wire", None, None, None),
            P("wire", None),
            P("wire", None),
            P("wire", None),
            P("wire", "col"),
        ),
        out_specs=P("wire", "col"),
        check_vma=False,
    )
```

```python
import math

import jax
import jax.numpy as jnp
from jax import lax
from jax.experimental import pallas as pl
from jax.experimental.layout import Layout, with_layout_constraint
from jax.experimental.pallas import tpu as pltpu
from jax.sharding import PartitionSpec as P


REACH = 2
F32 = jnp.float32
BF16 = jnp.bfloat16
F16 = jnp.float16


def split(value):
    high = lax.reduce_precision(value, 8, 7)
    return high.astype(BF16), (value - high).astype(BF16)


def dot(a, b):
    return jnp.dot(a, b, preferred_element_type=F32)


def dot_t(a, b):
    return lax.dot_general(a, b, (((0,), (0,)), ((), ())), preferred_element_type=F32)


def row_major(value):
    return with_layout_constraint(value, Layout(tuple(range(value.ndim))))


def band_kernel(picks_ref, core_ref, h_ref, x_ref, fetched_ref, swapped_ref, band_ref, pair_ref, tiles):
    blocks, slots, size, _ = h_ref.shape
    cols = x_ref.shape[1]
    reach = (tiles.shape[0] - blocks) // 2

    def put(at, ref, start, count):
        for k in range(count):
            tiles[at + k] = ref[start + k * size : start + (k + 1) * size]

    @pl.when(core_ref[0] == 0)
    def _():
        put(0, fetched_ref, 0, reach)
        put(reach + blocks, swapped_ref, 0, reach)

    @pl.when(core_ref[0] != 0)
    def _():
        put(0, swapped_ref, 0, reach)
        put(reach + blocks, fetched_ref, 0, reach)

    put(reach, x_ref, 0, blocks)

    @pl.loop(0, blocks, unroll=4)
    def _(j):
        total = dot(
            jnp.concatenate([h_ref[j, s] for s in range(slots)], axis=1),
            jnp.concatenate([tiles[picks_ref[j, s]] for s in range(slots)], axis=0),
        )
        rows = pl.ds(pl.multiple_of(j * size, size), size)
        high = total.astype(BF16)
        band_ref[rows, :] = total
        pair_ref[rows, :cols] = high
        pair_ref[rows, cols:] = (total - high.astype(F32)).astype(BF16)


def band_product(picks, core, hamiltonian, x, fetched, swapped):
    blocks, slots, size, _ = hamiltonian.shape
    rows, cols = x.shape
    vmem = pl.BlockSpec(memory_space=pltpu.VMEM)
    smem = pl.BlockSpec(memory_space=pltpu.SMEM)
    return pl.pallas_call(
        band_kernel,
        in_specs=[smem, smem, vmem, vmem, vmem, vmem],
        out_specs=[vmem, vmem],
        out_shape=[
            jax.ShapeDtypeStruct((rows, cols), F32),
            jax.ShapeDtypeStruct((rows, 2 * cols), BF16),
        ],
        scratch_shapes=[pltpu.VMEM((blocks + 2 * REACH, size, cols), BF16)],
        cost_estimate=pl.CostEstimate(
            flops=2 * slots * rows * size * cols, bytes_accessed=8 * rows * cols, transcendentals=0
        ),
        name="band",
    )(picks, core, hamiltonian, x, fetched, swapped)


class Cube:
    def __init__(self, chips, cores, orders):
        self.count = chips.bit_length() - 1
        me = lax.axis_index("wire")
        core = lax.axis_index("col") & 1
        self.perms = []
        self.bits = []
        for first, second in zip(*orders):
            axes = (first, second)
            self.perms.append(
                [
                    (w * cores + c, (w ^ (1 << axes[c & 1])) * cores + c)
                    for w in range(chips)
                    for c in range(cores)
                ]
            )
            self.bits.append((me >> jnp.where(core == 0, first, second)) & 1)

    def send(self, value, k):
        return lax.ppermute(value, ("wire", "col"), self.perms[k])

    def half(self, value, k, mine, axis=0):
        rows = value.shape[axis] // 2
        bit = self.bits[k] if mine else 1 - self.bits[k]
        return lax.dynamic_slice_in_dim(value, bit * rows, rows, axis)

    def reduce(self, value, got, start, wire_type, halved):
        for k in range(start, self.count):
            if k < halved:
                out = self.half(value, k, False)
                if got is not None:
                    out = out + self.half(got, k, False).astype(F32)
                out = out.astype(wire_type)
                value, got, out = lax.optimization_barrier((value, got, out))
                value = self.half(value, k, True)
                if got is not None:
                    value = value + self.half(got, k, True).astype(F32)
            else:
                if got is not None:
                    value = value + got.astype(F32)
                out = value.astype(wire_type)
            got = self.send(out, k)
        return value + got.astype(F32)

    def joined(self, value, got, k):
        return jnp.where(
            self.bits[k] == 0,
            jnp.concatenate([value, got], axis=0),
            jnp.concatenate([got, value], axis=0),
        )

    def gather(self, value, halved):
        for k in reversed(range(halved)):
            value = self.joined(value, self.send(value, k), k)
        return value


def steps(hamiltonian, offsets, phase_left, phase_right, orbitals):
    local_blocks = hamiltonian.shape[0]
    block_size = hamiltonian.shape[2]
    local_rows, cols = orbitals.shape
    rank = phase_left.shape[1]
    chips = lax.axis_size("wire")
    cores = lax.axis_size("col")
    total_rows = local_rows * chips
    count = chips.bit_length() - 1
    straight = list(range(count))
    crossed = list(range(count))
    first = list(straight)
    if count >= 3:
        first[1], first[2] = 2, 1
    if count >= 2:
        crossed[0], crossed[1] = 1, 0
    cube = Cube(chips, cores, (first, crossed))
    late = list(crossed)
    if count >= 4:
        late[2], late[3] = 3, 2
    small = Cube(chips, cores, (straight, late))
    swap = [(i, (i + 1) % cores) for i in range(cores)]

    scale = 2.0 ** -max(0, math.ceil(math.log2(36.0 * total_rows / 32768.0)))
    other = lax.ppermute(orbitals, "col", swap)

    def part(mine):
        right = cube.half(phase_right, 0, mine, axis=1)
        left = jnp.where((cube.bits[0] == 0) == mine, orbitals, other)
        return dot_t(right, orbitals), dot_t(left, orbitals) * scale

    away = jnp.concatenate([z.astype(F16) for z in part(False)], axis=0)
    got = cube.send(away, 0)
    here = jnp.concatenate(part(True), axis=0)
    halved = count - 1
    mine = cube.reduce(here, got, 1, F16, halved)

    width = REACH * block_size
    core = lax.axis_index("col") & 1
    ring = []
    for w in range(chips):
        for c in range(cores):
            ring.append((w * cores + c, (w + 1 - 2 * (c & 1)) % chips * cores + c))
    edge = jnp.concatenate(
        [
            jnp.where(core == 0, z[local_rows - width :], z[:width])
            for z in (orbitals, other)
        ],
        axis=0,
    )
    fetched = lax.ppermute(edge, ("wire", "col"), ring)
    swapped = lax.ppermute(fetched[width:], "col", swap)
    own_late, other_late, _ = lax.optimization_barrier((orbitals, other, away))
    both = jnp.concatenate([own_late, other_late], axis=1)
    offsets_late, _ = lax.optimization_barrier((offsets, away))
    picks = jnp.arange(local_blocks, dtype=jnp.int32)[:, None] + offsets_late + REACH
    band, pair = band_product(picks, core[None], hamiltonian, orbitals, fetched, swapped)
    cross_band = dot_t(both, pair)
    cross_band = cross_band[:, :cols] + cross_band[:, cols:]
    half_rank = rank // 2
    left_scale = 2.0 ** -max(0, math.ceil(math.log2(0.75 * local_rows / 32768.0)))
    left_away = (dot_t(both, cube.half(phase_left, 0, False, axis=1)) * left_scale).astype(F16)
    left_got = cube.send(left_away, 0)
    left_here = lax.optimization_barrier(dot_t(both, cube.half(phase_left, 0, True, axis=1)))
    left = split(left_here + left_got.astype(F32) * (1.0 / left_scale))
    left_high, left_low = lax.optimization_barrier(left)

    start = jnp.int32(0)
    span = here.shape[0]
    for bit in cube.bits[1:halved]:
        span //= 2
        start = start + bit * span
    row = start + lax.broadcasted_iota(jnp.int32, (mine.shape[0], 1), 0)
    mine = jnp.where(row < half_rank, lax.reduce_precision(mine, 8, 7), mine).astype(F16)
    for k in reversed(range(1, halved)):
        mine = cube.joined(mine, cube.send(mine, k), k)
    factor = mine[:half_rank].astype(BF16)
    cross_part = cross_band + dot(left_high, factor) + dot(left_low, factor)
    got = cube.send(mine, 0)
    low, top = jnp.where(cube.bits[0] == 0, mine, got), jnp.where(cube.bits[0] == 0, got, mine)
    coupling = jnp.concatenate([low[:half_rank], top[:half_rank]], axis=0).astype(BF16)
    inter = [z[half_rank:].astype(F32) * (1.0 / (scale * total_rows)) for z in (low, top)]

    halved = min(2, count)
    cross = small.gather(small.reduce(cross_part, None, 0, F32, halved), halved)
    cross = cross * (1.0 / total_rows)

    half_rows = local_rows // 2
    pieces = [slice(k * half_rows, (k + 1) * half_rows) for k in range(2)]
    image = []
    image_other = []
    factor = coupling
    for rows_k in pieces:
        pair_k = split(band[rows_k] + dot(phase_left[rows_k], factor))
        *pair_k, factor = lax.optimization_barrier((*pair_k, factor))
        image.append(pair_k)
    for value in image:
        image_other.append([lax.ppermute(z, "col", swap) for z in value])
    eye = (lax.broadcasted_iota(jnp.int32, (cols, cols), 0) == lax.broadcasted_iota(jnp.int32, (cols, cols), 1))
    weights = [split(w) for w in (2.0 * eye.astype(F32) - inter[0], -inter[1])]

    def weighed(value, weight):
        return dot(value[0], weight[0]) + dot(value[1], weight[0]) + dot(value[0], weight[1])

    base = [weighed(z, weights[0]) for z in image]
    base = [z + weighed(o, weights[1]) for z, o in zip(base, image_other)]
    high, low = split(cross)
    base = jnp.concatenate(base, axis=0)
    return row_major(base - (dot(both, high) + dot(both, low)))


def solution(mesh):
    return jax.shard_map(
        steps,
        mesh=mesh,
        in_specs=(
            P("wire", None, None, None),
            P("wire", None),
            P("wire", None),
            P("wire", None),
            P("wire", "col"),
        ),
        out_specs=P("wire", "col"),
        check_vma=False,
    )
```

```python
import math

import jax
import jax.numpy as jnp
from jax import lax
from jax.experimental import pallas as pl
from jax.experimental.layout import Layout, with_layout_constraint
from jax.experimental.pallas import tpu as pltpu
from jax.sharding import PartitionSpec as P


REACH = 2
F32 = jnp.float32
BF16 = jnp.bfloat16
F16 = jnp.float16


def split(value):
    high = lax.reduce_precision(value, 8, 7)
    return high.astype(BF16), (value - high).astype(BF16)


def dot(a, b):
    return jnp.dot(a, b, preferred_element_type=F32)


def dot_t(a, b):
    return lax.dot_general(a, b, (((0,), (0,)), ((), ())), preferred_element_type=F32)


def row_major(value):
    return with_layout_constraint(value, Layout(tuple(range(value.ndim))))


def band_kernel(picks_ref, core_ref, h_ref, x_ref, fetched_ref, swapped_ref, band_ref, pair_ref, tiles):
    blocks, slots, size, _ = h_ref.shape
    cols = x_ref.shape[1]
    reach = (tiles.shape[0] - blocks) // 2

    def put(at, ref, start, count):
        for k in range(count):
            tiles[at + k] = ref[start + k * size : start + (k + 1) * size]

    @pl.when(core_ref[0] == 0)
    def _():
        put(0, fetched_ref, 0, reach)
        put(reach + blocks, swapped_ref, 0, reach)

    @pl.when(core_ref[0] != 0)
    def _():
        put(0, swapped_ref, 0, reach)
        put(reach + blocks, fetched_ref, 0, reach)

    put(reach, x_ref, 0, blocks)

    @pl.loop(0, blocks, unroll=4)
    def _(j):
        total = dot(
            jnp.concatenate([h_ref[j, s] for s in range(slots)], axis=1),
            jnp.concatenate([tiles[picks_ref[j, s]] for s in range(slots)], axis=0),
        )
        rows = pl.ds(pl.multiple_of(j * size, size), size)
        high = total.astype(BF16)
        band_ref[rows, :] = total
        pair_ref[rows, :cols] = high
        pair_ref[rows, cols:] = (total - high.astype(F32)).astype(BF16)


def band_product(picks, core, hamiltonian, x, fetched, swapped):
    blocks, slots, size, _ = hamiltonian.shape
    rows, cols = x.shape
    vmem = pl.BlockSpec(memory_space=pltpu.VMEM)
    smem = pl.BlockSpec(memory_space=pltpu.SMEM)
    return pl.pallas_call(
        band_kernel,
        in_specs=[smem, smem, vmem, vmem, vmem, vmem],
        out_specs=[vmem, vmem],
        out_shape=[
            jax.ShapeDtypeStruct((rows, cols), F32),
            jax.ShapeDtypeStruct((rows, 2 * cols), BF16),
        ],
        scratch_shapes=[pltpu.VMEM((blocks + 2 * REACH, size, cols), BF16)],
        cost_estimate=pl.CostEstimate(
            flops=2 * slots * rows * size * cols, bytes_accessed=8 * rows * cols, transcendentals=0
        ),
        name="band",
    )(picks, core, hamiltonian, x, fetched, swapped)


class Cube:
    def __init__(self, chips, cores, orders):
        self.count = chips.bit_length() - 1
        me = lax.axis_index("wire")
        core = lax.axis_index("col") & 1
        self.perms = []
        self.bits = []
        for first, second in zip(*orders):
            axes = (first, second)
            self.perms.append(
                [
                    (w * cores + c, (w ^ (1 << axes[c & 1])) * cores + c)
                    for w in range(chips)
                    for c in range(cores)
                ]
            )
            self.bits.append((me >> jnp.where(core == 0, first, second)) & 1)

    def send(self, value, k):
        return lax.ppermute(value, ("wire", "col"), self.perms[k])

    def half(self, value, k, mine, axis=0):
        rows = value.shape[axis] // 2
        bit = self.bits[k] if mine else 1 - self.bits[k]
        return lax.dynamic_slice_in_dim(value, bit * rows, rows, axis)

    def reduce(self, value, got, start, wire_type, halved):
        for k in range(start, self.count):
            if k < halved:
                out = self.half(value, k, False)
                if got is not None:
                    out = out + self.half(got, k, False).astype(F32)
                out = out.astype(wire_type)
                value, got, out = lax.optimization_barrier((value, got, out))
                value = self.half(value, k, True)
                if got is not None:
                    value = value + self.half(got, k, True).astype(F32)
            else:
                if got is not None:
                    value = value + got.astype(F32)
                out = value.astype(wire_type)
            got = self.send(out, k)
        return value + got.astype(F32)

    def joined(self, value, got, k):
        return jnp.where(
            self.bits[k] == 0,
            jnp.concatenate([value, got], axis=0),
            jnp.concatenate([got, value], axis=0),
        )

    def gather(self, value, halved):
        for k in reversed(range(halved)):
            value = self.joined(value, self.send(value, k), k)
        return value


def steps(hamiltonian, offsets, phase_left, phase_right, orbitals):
    local_blocks = hamiltonian.shape[0]
    block_size = hamiltonian.shape[2]
    local_rows, cols = orbitals.shape
    rank = phase_left.shape[1]
    chips = lax.axis_size("wire")
    cores = lax.axis_size("col")
    total_rows = local_rows * chips
    count = chips.bit_length() - 1
    straight = list(range(count))
    crossed = list(range(count))
    first = list(straight)
    if count >= 3:
        first[1], first[2] = 2, 1
    if count >= 2:
        crossed[0], crossed[1] = 1, 0
    cube = Cube(chips, cores, (first, crossed))
    late = list(crossed)
    if count >= 4:
        late[2], late[3] = 3, 2
    small = Cube(chips, cores, (straight, late))
    swap = [(i, (i + 1) % cores) for i in range(cores)]

    scale = 2.0 ** -max(0, math.ceil(math.log2(36.0 * total_rows / 32768.0)))
    other = lax.ppermute(orbitals, "col", swap)

    def part(mine):
        right = cube.half(phase_right, 0, mine, axis=1)
        left = jnp.where((cube.bits[0] == 0) == mine, orbitals, other)
        return dot_t(right, orbitals), dot_t(left, orbitals) * scale

    away = jnp.concatenate([z.astype(F16) for z in part(False)], axis=0)
    got = cube.send(away, 0)
    here = jnp.concatenate(part(True), axis=0)
    halved = count - 1
    mine = cube.reduce(here, got, 1, F16, halved)

    width = REACH * block_size
    core = lax.axis_index("col") & 1
    ring = []
    for w in range(chips):
        for c in range(cores):
            ring.append((w * cores + c, (w + 1 - 2 * (c & 1)) % chips * cores + c))
    edge = jnp.concatenate(
        [
            jnp.where(core == 0, z[local_rows - width :], z[:width])
            for z in (orbitals, other)
        ],
        axis=0,
    )
    fetched = lax.ppermute(edge, ("wire", "col"), ring)
    swapped = lax.ppermute(fetched[width:], "col", swap)
    own_late, other_late, _ = lax.optimization_barrier((orbitals, other, away))
    both = jnp.concatenate([own_late, other_late], axis=1)
    offsets_late, _ = lax.optimization_barrier((offsets, away))
    picks = jnp.arange(local_blocks, dtype=jnp.int32)[:, None] + offsets_late + REACH
    band, pair = band_product(picks, core[None], hamiltonian, orbitals, fetched, swapped)
    cross_band = dot_t(both, pair)
    cross_band = cross_band[:, :cols] + cross_band[:, cols:]
    half_rank = rank // 2
    left_scale = 2.0 ** -max(0, math.ceil(math.log2(0.75 * local_rows / 32768.0)))
    left_away = (dot_t(both, cube.half(phase_left, 0, False, axis=1)) * left_scale).astype(F16)
    left_got = cube.send(left_away, 0)
    left_here = lax.optimization_barrier(dot_t(both, cube.half(phase_left, 0, True, axis=1)))
    left = split(left_here + left_got.astype(F32) * (1.0 / left_scale))
    left_high, left_low = lax.optimization_barrier(left)

    start = jnp.int32(0)
    span = here.shape[0]
    for bit in cube.bits[1:halved]:
        span //= 2
        start = start + bit * span
    row = start + lax.broadcasted_iota(jnp.int32, (mine.shape[0], 1), 0)
    mine = jnp.where(row < half_rank, lax.reduce_precision(mine, 8, 7), mine).astype(F16)
    for k in reversed(range(1, halved)):
        mine = cube.joined(mine, cube.send(mine, k), k)
    factor = mine[:half_rank].astype(BF16)
    cross_part = cross_band + dot(left_high, factor) + dot(left_low, factor)
    image = band + dot(cube.half(phase_left, 0, True, axis=1), factor)
    got = cube.send(mine, 0)
    lower = cube.bits[0] == 0
    inter = [
        z.astype(F32) * (1.0 / (scale * total_rows))
        for z in (
            jnp.where(lower, mine[half_rank:], got[half_rank:]),
            jnp.where(lower, got[half_rank:], mine[half_rank:]),
        )
    ]

    halved = min(2, count)
    cross = small.gather(small.reduce(cross_part, None, 0, F32, halved), halved)
    cross = cross * (1.0 / total_rows)

    factor = got[:half_rank].astype(BF16)
    image = split(image + dot(cube.half(phase_left, 0, False, axis=1), factor))
    image_other = [lax.ppermute(z, "col", swap) for z in image]
    eye = (lax.broadcasted_iota(jnp.int32, (cols, cols), 0) == lax.broadcasted_iota(jnp.int32, (cols, cols), 1))
    weights = [split(w) for w in (2.0 * eye.astype(F32) - inter[0], -inter[1])]

    def weighed(value, weight):
        return dot(value[0], weight[0]) + dot(value[1], weight[0]) + dot(value[0], weight[1])

    base = weighed(image, weights[0])
    base = base + weighed(image_other, weights[1])
    high, low = split(cross)
    return row_major(base - (dot(both, high) + dot(both, low)))


def solution(mesh):
    return jax.shard_map(
        steps,
        mesh=mesh,
        in_specs=(
            P("wire", None, None, None),
            P("wire", None),
            P("wire", None),
            P("wire", None),
            P("wire", "col"),
        ),
        out_specs=P("wire", "col"),
        check_vma=False,
    )
```

```python
import math

import jax
import jax.numpy as jnp
from jax import lax
from jax.experimental import pallas as pl
from jax.experimental.layout import Layout, with_layout_constraint
from jax.experimental.pallas import tpu as pltpu
from jax.sharding import PartitionSpec as P


REACH = 2
F32 = jnp.float32
BF16 = jnp.bfloat16
F16 = jnp.float16


def split(value):
    high = lax.reduce_precision(value, 8, 7)
    return high.astype(BF16), (value - high).astype(BF16)


def dot(a, b):
    return jnp.dot(a, b, preferred_element_type=F32)


def dot_t(a, b):
    return lax.dot_general(a, b, (((0,), (0,)), ((), ())), preferred_element_type=F32)


def row_major(value):
    return with_layout_constraint(value, Layout(tuple(range(value.ndim))))


def band_kernel(picks_ref, core_ref, h_ref, x_ref, fetched_ref, swapped_ref, band_ref, pair_ref, tiles):
    blocks, slots, size, _ = h_ref.shape
    cols = x_ref.shape[1]
    reach = (tiles.shape[0] - blocks) // 2

    def put(at, ref, start, count):
        for k in range(count):
            tiles[at + k] = ref[start + k * size : start + (k + 1) * size]

    @pl.when(core_ref[0] == 0)
    def _():
        put(0, fetched_ref, 0, reach)
        put(reach + blocks, swapped_ref, 0, reach)

    @pl.when(core_ref[0] != 0)
    def _():
        put(0, swapped_ref, 0, reach)
        put(reach + blocks, fetched_ref, 0, reach)

    put(reach, x_ref, 0, blocks)

    @pl.loop(0, blocks, unroll=4)
    def _(j):
        total = dot(
            jnp.concatenate([h_ref[j, s] for s in range(slots)], axis=1),
            jnp.concatenate([tiles[picks_ref[j, s]] for s in range(slots)], axis=0),
        )
        rows = pl.ds(pl.multiple_of(j * size, size), size)
        high = total.astype(BF16)
        band_ref[rows, :] = total
        pair_ref[rows, :cols] = high
        pair_ref[rows, cols:] = (total - high.astype(F32)).astype(BF16)


def band_product(picks, core, hamiltonian, x, fetched, swapped):
    blocks, slots, size, _ = hamiltonian.shape
    rows, cols = x.shape
    vmem = pl.BlockSpec(memory_space=pltpu.VMEM)
    smem = pl.BlockSpec(memory_space=pltpu.SMEM)
    return pl.pallas_call(
        band_kernel,
        in_specs=[smem, smem, vmem, vmem, vmem, vmem],
        out_specs=[vmem, vmem],
        out_shape=[
            jax.ShapeDtypeStruct((rows, cols), F32),
            jax.ShapeDtypeStruct((rows, 2 * cols), BF16),
        ],
        scratch_shapes=[pltpu.VMEM((blocks + 2 * REACH, size, cols), BF16)],
        cost_estimate=pl.CostEstimate(
            flops=2 * slots * rows * size * cols, bytes_accessed=8 * rows * cols, transcendentals=0
        ),
        name="band",
    )(picks, core, hamiltonian, x, fetched, swapped)


class Cube:
    def __init__(self, chips, cores, orders):
        self.count = chips.bit_length() - 1
        me = lax.axis_index("wire")
        core = lax.axis_index("col") & 1
        self.perms = []
        self.bits = []
        for first, second in zip(*orders):
            axes = (first, second)
            self.perms.append(
                [
                    (w * cores + c, (w ^ (1 << axes[c & 1])) * cores + c)
                    for w in range(chips)
                    for c in range(cores)
                ]
            )
            self.bits.append((me >> jnp.where(core == 0, first, second)) & 1)

    def send(self, value, k):
        return lax.ppermute(value, ("wire", "col"), self.perms[k])

    def half(self, value, k, mine, axis=0):
        rows = value.shape[axis] // 2
        bit = self.bits[k] if mine else 1 - self.bits[k]
        return lax.dynamic_slice_in_dim(value, bit * rows, rows, axis)

    def reduce(self, value, got, start, wire_type, halved):
        for k in range(start, self.count):
            if k < halved:
                out = self.half(value, k, False)
                if got is not None:
                    out = out + self.half(got, k, False).astype(F32)
                out = out.astype(wire_type)
                value, got, out = lax.optimization_barrier((value, got, out))
                value = self.half(value, k, True)
                if got is not None:
                    value = value + self.half(got, k, True).astype(F32)
            else:
                if got is not None:
                    value = value + got.astype(F32)
                out = value.astype(wire_type)
            got = self.send(out, k)
        return value + got.astype(F32)

    def joined(self, value, got, k):
        return jnp.where(
            self.bits[k] == 0,
            jnp.concatenate([value, got], axis=0),
            jnp.concatenate([got, value], axis=0),
        )

    def gather(self, value, halved):
        for k in reversed(range(halved)):
            value = self.joined(value, self.send(value, k), k)
        return value


def steps(hamiltonian, offsets, phase_left, phase_right, orbitals):
    local_blocks = hamiltonian.shape[0]
    block_size = hamiltonian.shape[2]
    local_rows, cols = orbitals.shape
    rank = phase_left.shape[1]
    chips = lax.axis_size("wire")
    cores = lax.axis_size("col")
    total_rows = local_rows * chips
    count = chips.bit_length() - 1
    straight = list(range(count))
    crossed = list(range(count))
    first = list(straight)
    if count >= 3:
        first[1], first[2] = 2, 1
    if count >= 2:
        crossed[0], crossed[1] = 1, 0
    cube = Cube(chips, cores, (first, crossed))
    late = list(crossed)
    if count >= 4:
        late[2], late[3] = 3, 2
    small = Cube(chips, cores, (straight, late))
    swap = [(i, (i + 1) % cores) for i in range(cores)]

    scale = 2.0 ** -max(0, math.ceil(math.log2(36.0 * total_rows / 32768.0)))
    other = lax.ppermute(orbitals, "col", swap)

    def part(mine):
        right = cube.half(phase_right, 0, mine, axis=1)
        left = jnp.where((cube.bits[0] == 0) == mine, orbitals, other)
        return dot_t(right, orbitals), dot_t(left, orbitals) * scale

    away = jnp.concatenate([z.astype(F16) for z in part(False)], axis=0)
    got = cube.send(away, 0)
    here = jnp.concatenate(part(True), axis=0)
    halved = count - 1
    mine = cube.reduce(here, got, 1, F16, halved)

    width = REACH * block_size
    core = lax.axis_index("col") & 1
    ring = []
    for w in range(chips):
        for c in range(cores):
            ring.append((w * cores + c, (w + 1 - 2 * (c & 1)) % chips * cores + c))
    edge = jnp.concatenate(
        [
            jnp.where(core == 0, z[local_rows - width :], z[:width])
            for z in (orbitals, other)
        ],
        axis=0,
    )
    fetched = lax.ppermute(edge, ("wire", "col"), ring)
    swapped = lax.ppermute(fetched[width:], "col", swap)
    own_late, other_late, _ = lax.optimization_barrier((orbitals, other, away))
    both = jnp.concatenate([own_late, other_late], axis=1)
    offsets_late, _ = lax.optimization_barrier((offsets, away))
    picks = jnp.arange(local_blocks, dtype=jnp.int32)[:, None] + offsets_late + REACH
    band, pair = band_product(picks, core[None], hamiltonian, orbitals, fetched, swapped)
    cross_band = dot_t(both, pair)
    cross_band = cross_band[:, :cols] + cross_band[:, cols:]
    half_rank = rank // 2
    left_scale = 2.0 ** -max(0, math.ceil(math.log2(0.75 * local_rows / 32768.0)))
    left_away = (dot_t(both, cube.half(phase_left, 0, False, axis=1)) * left_scale).astype(F16)
    left_got = cube.send(left_away, 0)
    left_here = lax.optimization_barrier(dot_t(both, cube.half(phase_left, 0, True, axis=1)))
    left = split(left_here + left_got.astype(F32) * (1.0 / left_scale))
    left_high, left_low = lax.optimization_barrier(left)

    start = jnp.int32(0)
    span = here.shape[0]
    for bit in cube.bits[1:halved]:
        span //= 2
        start = start + bit * span
    row = start + lax.broadcasted_iota(jnp.int32, (mine.shape[0], 1), 0)
    mine = jnp.where(row < half_rank, lax.reduce_precision(mine, 8, 7), mine).astype(F16)
    for k in reversed(range(1, halved)):
        mine = cube.joined(mine, cube.send(mine, k), k)
    factor = mine[:half_rank].astype(BF16)
    cross_part = cross_band + dot(left_high, factor) + dot(left_low, factor)
    image = dot(cube.half(phase_left, 0, True, axis=1), factor)
    got = cube.send(mine, 0)
    lower = cube.bits[0] == 0
    inter = [
        z.astype(F32) * (1.0 / (scale * total_rows))
        for z in (
            jnp.where(lower, mine[half_rank:], got[half_rank:]),
            jnp.where(lower, got[half_rank:], mine[half_rank:]),
        )
    ]

    halved = min(2, count)
    cross = small.gather(small.reduce(cross_part, None, 0, F32, halved), halved)
    cross = cross * (1.0 / total_rows)

    factor = got[:half_rank].astype(BF16)
    half_rows = local_rows // 2
    halves = []
    halves_other = []
    for k in range(2):
        rows_left = lax.dynamic_slice(
            phase_left,
            (k * half_rows, (1 - cube.bits[0]) * half_rank),
            (half_rows, half_rank),
        )
        span = slice(k * half_rows, (k + 1) * half_rows)
        value = split(band[span] + image[span] + dot(rows_left, factor))
        *value, factor = lax.optimization_barrier((*value, factor))
        halves.append(value)
    for value in halves:
        halves_other.append([lax.ppermute(z, "col", swap) for z in value])
    eye = (lax.broadcasted_iota(jnp.int32, (cols, cols), 0) == lax.broadcasted_iota(jnp.int32, (cols, cols), 1))
    weights = [split(w) for w in (2.0 * eye.astype(F32) - inter[0], -inter[1])]

    def weighed(value, weight):
        return dot(value[0], weight[0]) + dot(value[1], weight[0]) + dot(value[0], weight[1])

    base = [weighed(z, weights[0]) for z in halves]
    base = [z + weighed(o, weights[1]) for z, o in zip(base, halves_other)]
    base = jnp.concatenate(base, axis=0)
    high, low = split(cross)
    return row_major(base - (dot(both, high) + dot(both, low)))


def solution(mesh):
    return jax.shard_map(
        steps,
        mesh=mesh,
        in_specs=(
            P("wire", None, None, None),
            P("wire", None),
            P("wire", None),
            P("wire", None),
            P("wire", "col"),
        ),
        out_specs=P("wire", "col"),
        check_vma=False,
    )
```
